32 devices in a mesh: view: 4 (over x, core), gy: 2 (over y), gz: 4 (over z).
Axes of the slice: x: 2, y: 2, z: 4, core: 2. Of those that a mesh axis runs over, the one named last changes fastest.
Arguments:
- estimate: float32 [16, 128, 1024], P('view', 'gy', 'gz'), may hold values from 0.5 to 2
- view_data: bfloat16 [8, 16, 128, 1024], P('view', None, 'gy', 'gz'), may hold values from 0.25 to 2
- block_scales: float32 [8, 4, 16], P('view', 'gy', 'gz'), may hold values from 0.5 to 2
- block_flags: int32 [8, 4, 16], P('view', 'gy', 'gz'), may hold values 0 or 1
- profile: float32 [8, 3, 33], P('view'), may hold values from 0.05 to 1
- supports: int32 [8, 3], P('view'), may hold values from 1 to 16, as said below
Outputs:
- refined: float32 [16, 128, 1024], P('view', 'gy', 'gz')
The draws below stay inside these ranges and needn't reach their ends.
Inputs may be any that keep to these rules, and one draw needn't show every extreme that they name: supports[v] holds view v's half-widths along x, y and z: along x 1 to 6, along y and z 1 to 16; some view has 6 along x, some view 16 along y and some view 16 along z. block_flags[v, b, c] is 1 where view v's data in the block of 32 x 64 cells (b, c) are valid.
All inputs are finite; a program needn't handle non-finite values.
Results may differ from the reference program's by a relative error of at most 0.0003.
Values sent between devices are 32-bit elements; how exact they have to be, the bound alone decides.
A program may use at most 64 MiB of HBM per device.

```python
import math
import jax
import jax.numpy as jnp
from jax import lax

R = 16
RX = 6
NX = 16
BY = 32
BZ = 64
ITERS = 2
VIEWS = 8
NY = 128
NZ = 1024


def draw_supports(key, part):
    key_list = jax.random.split(jax.random.fold_in(key, 11), 3)
    along_planes = jax.random.randint(key_list[0], (VIEWS, 1), 1, RX + 1)
    along_cells = jax.random.randint(key_list[1], (VIEWS, 2), 1, R + 1)
    chosen = jax.random.randint(key_list[2], (3,), 0, VIEWS)
    row_index = jnp.arange(VIEWS)[:, None]
    col_index = jnp.arange(2)[None, :]
    along_planes = jnp.where(row_index == chosen[0], RX, along_planes)
    along_cells = jnp.where((row_index == chosen[1]) & (col_index == 0), R, along_cells)
    along_cells = jnp.where((row_index == chosen[2]) & (col_index == 1), R, along_cells)
    return jnp.concatenate([along_planes, along_cells], axis=1).astype(jnp.int32)


def set_ends(array, rng, least, high):
    dims = array.shape
    place = [jax.random.randint(jax.random.fold_in(rng, axis), (), 0, dims[axis]) for axis in range(len(dims))]
    array = array.at[tuple(place)].set(least)
    longest = dims.index(max(dims))
    place[longest] = (place[longest] + 1) % dims[longest]
    return array.at[tuple(place)].set(high)


def levels(own_key, shape, pieces, least, top_value):
    level, own = 1.0, jax.random.fold_in(own_key, 6)
    for axis_at, parts in pieces:
        steps = jnp.exp(jax.random.uniform(jax.random.fold_in(own, axis_at), (parts,), jnp.float32, least / len(pieces), top_value / len(pieces)))
        level = level * jnp.repeat(steps, shape[axis_at] // parts).reshape([-1 if axis == axis_at else 1 for axis in range(len(shape))])
    return level


def setup_inputs(seed: int = 0) -> dict:
    seeds = jax.random.split(jax.random.key(seed), 7)
    estimate = jnp.clip(0.5 + 1.5 * jax.random.uniform(seeds[0], (NX, NY, NZ), jnp.float32) ** levels(seeds[0], (NX, NY, NZ), ((0, 4), (1, 2), (2, 4)), -0.2, 0.2), 0.5, 2.0)
    view_data = jnp.clip(0.25 + 1.75 * jax.random.uniform(seeds[1], (VIEWS, NX, NY, NZ), jnp.float32) ** levels(seeds[1], (VIEWS, NX, NY, NZ), ((0, 4), (2, 2), (3, 4)), -0.2, 0.2), 0.25, 2.0).astype(jnp.bfloat16)
    block_scales = jnp.clip(jnp.exp(math.log(2.0) - 1.3862944 * jax.random.uniform(seeds[2], (VIEWS, NY // BY, NZ // BZ), jnp.float32) ** levels(seeds[2], (VIEWS, NY // BY, NZ // BZ), ((0, 4), (1, 2), (2, 4)), -0.2, 0.2)), 0.5, 2.0)
    block_flags = set_ends((jax.random.randint(seeds[3], (VIEWS, NY // BY, NZ // BZ), 0, 4) < 3).astype(jnp.int32), jax.random.fold_in(seeds[3], 1), 0, 1)
    profile = jnp.clip(jnp.exp(math.log(1.0) - 2.9957323 * jax.random.uniform(seeds[4], (VIEWS, 3, 2 * R + 1), jnp.float32) ** levels(seeds[4], (VIEWS, 3, 2 * R + 1), ((0, 4),), -0.2, 0.2)), 0.05, 1.0)
    supports = draw_supports(jax.random.fold_in(seeds[6], 71), 0)
    return {"estimate": estimate, "view_data": view_data, "block_scales": block_scales, "block_flags": block_flags, "profile": profile, "supports": supports}


def band_matrix(tap_table, row_count, col_count, offset):
    row_index = lax.broadcasted_iota(jnp.int32, (row_count, col_count), 0)
    col_index = lax.broadcasted_iota(jnp.int32, (row_count, col_count), 1)
    lag_index = row_index - col_index + offset

    def place_tap(tap_index, summed):
        return jnp.where(lag_index == tap_index, tap_table[tap_index], summed)

    return lax.fori_loop(0, tap_table.shape[0], place_tap, jnp.zeros((row_count, col_count), jnp.float32))


def kernel_table(profile, supports):
    tap_count = profile.shape[-1]
    distance = jnp.abs(jnp.arange(tap_count, dtype=jnp.int32) - (tap_count - 1) // 2)
    inside = distance[None, None, :] <= supports[:, :, None]
    masked = jnp.where(inside, profile, 0.0)
    return masked / jnp.sum(masked, axis=-1, keepdims=True)


def blur_axis(field, kernel, axis):
    half_width = (kernel.shape[0] - 1) // 2
    tile_size = 2 * half_width
    rotated = jnp.moveaxis(field, axis, -1)
    length = rotated.shape[-1]
    padded = jnp.pad(rotated, [(0, 0)] * (rotated.ndim - 1) + [(half_width, half_width)])
    blocks = padded.reshape(rotated.shape[:-1] + (length // tile_size + 1, tile_size))
    band_full = band_matrix(kernel, 2 * tile_size, tile_size, 0)
    leading = jnp.einsum('...bj,ji->...bi', blocks[..., :-1, :], band_full[:tile_size], precision=lax.Precision.HIGHEST)
    second = jnp.einsum('...bj,ji->...bi', blocks[..., 1:, :], band_full[tile_size:], precision=lax.Precision.HIGHEST)
    return jnp.moveaxis((leading + second).reshape(rotated.shape), -1, axis)


def blur(field, kernel_rows):
    half_width = (kernel_rows.shape[1] - 1) // 2
    planes = field.shape[0]
    plane_band = band_matrix(kernel_rows[0], planes, planes, half_width)
    mixed_planes = jnp.einsum('jyz,ji->iyz', field, plane_band, precision=lax.Precision.HIGHEST)
    along_rows = blur_axis(mixed_planes, kernel_rows[1], 1)
    return blur_axis(along_rows, kernel_rows[2], 2)


def reference(estimate, view_data, block_scales, block_flags, profile, supports):
    forward = kernel_table(profile, supports)
    backward = forward[:, :, ::-1]
    view_count = view_data.shape[0]
    current = estimate
    for iteration in range(ITERS):
        def add_view(view_index, totals):
            blurred = blur(current, forward[view_index])
            scale_map = jnp.repeat(jnp.repeat(block_scales[view_index], BY, axis=0), BZ, axis=1)
            valid_map = jnp.repeat(jnp.repeat(block_flags[view_index], BY, axis=0), BZ, axis=1)
            measured = view_data[view_index].astype(jnp.float32) * scale_map[None]
            ratios = jnp.where(valid_map[None] == 1, measured / blurred, 1.0)
            return totals + blur(ratios, backward[view_index])

        corrections = lax.fori_loop(0, view_count, add_view, jnp.zeros(current.shape, jnp.float32))
        current = current * corrections / view_count
    return current
```

```python
import functools

import jax
import jax.numpy as jnp
from jax import lax
from jax.experimental import pallas as pl
from jax.experimental.pallas import tpu as pltpu
from jax.sharding import PartitionSpec as P

BY = 32
BZ = 64
ITERS = 2
LANES = 128
MESH = pl.DeviceIdType.MESH
BF = jnp.bfloat16
F32 = jnp.float32


def kernel_table(profile, supports):
    tap_count = profile.shape[-1]
    distance = jnp.abs(jnp.arange(tap_count, dtype=jnp.int32) - (tap_count - 1) // 2)
    inside = distance[None, None, :] <= supports[:, :, None]
    masked = jnp.where(inside, profile, 0.0)
    return masked / jnp.sum(masked, axis=-1, keepdims=True)


def lane_iota(rows):
    return lax.broadcasted_iota(jnp.int32, (rows, LANES), 1)


def toeplitz(row, rows, shift):
    wide = jnp.broadcast_to(row, (rows, LANES))
    return pltpu.roll(wide, shift % LANES, 1, stride=1, stride_axis=0)


def roll_lanes(x, shift):
    shift = shift % LANES
    return pltpu.roll(x, shift, 1) if shift else x


def build_plane_row(dst, row_base, kx, ky, planes, hw):
    lane = lane_iota(hw)
    per_tile = LANES // hw
    halves = planes // per_tile
    tall = toeplitz(ky, hw, 0)
    bands = []
    for d in range(3):
        q = jnp.where(lane < hw, roll_lanes(tall, -hw * d), 0.0)
        width = hw
        while width < LANES:
            q = q + roll_lanes(q, width)
            width *= 2
        bands.append(q)
    tx = toeplitz(kx, planes, -hw)
    row_id = lax.broadcasted_iota(jnp.int32, (LANES, LANES), 0)
    group = lax.broadcasted_iota(jnp.int32, (LANES, LANES), 1) // hw
    for half in range(halves):
        pick = (row_id == group + half * per_tile).astype(F32)
        spread = jnp.dot(tx, pick, precision=lax.Precision.HIGHEST, preferred_element_type=F32)
        for d in range(3):
            for x in range(planes):
                tile = spread[x : x + 1, :] * bands[d]
                c0 = (halves * d + half) * LANES
                dst[row_base + x * hw : row_base + (x + 1) * hw, c0 : c0 + LANES] = tile.astype(BF)


def build_depth(dst, v, kz, rows_z, hw):
    row_j = lax.broadcasted_iota(jnp.int32, (rows_z, LANES), 0)
    lane = lane_iota(rows_z)
    reps = rows_z // LANES
    t = jnp.concatenate([toeplitz(kz, LANES, -hw)] * reps, axis=0)
    for ct in range(reps):
        c = lane + ct * LANES
        keep = jnp.abs(c - row_j) <= hw
        dst[v, :, ct * LANES : (ct + 1) * LANES] = jnp.where(keep, t, 0.0).astype(BF)
    h = jnp.concatenate([toeplitz(kz, LANES, 0)] * reps, axis=0)
    low = (row_j < hw) & (lane < hw)
    high = (row_j >= rows_z - hw) & (lane >= hw) & (lane < 2 * hw)
    h = jnp.where(low | high, h, 0.0)
    width = 2 * hw
    while width < LANES:
        h = h + roll_lanes(h, width)
        width *= 2
    dst[v, :, rows_z : rows_z + LANES] = h.astype(BF)


def kernel(
    sizes, est, vd, scales, flags, taps, out,
    fg, pk, wk, wl, wr, fb, am, bm, mt, gp, ob, zp,
    r1, r1z, s2, s2z, r2, r2z, ub, zu, zl, zr, yu, yd, ssem, rsem,
):
    ny, nz, views, planes, rows_y, rows_z, own, hw = sizes
    nb = rows_y // hw
    ne = nb + 2
    blk = planes * hw
    v = lax.axis_index("view")
    gy = lax.axis_index("gy")
    gz = lax.axis_index("gz")
    va, vb, vc = (lax.bitwise_xor(v, 1), lax.bitwise_xor(v, 2), lax.bitwise_xor(v, 3))
    has_up, has_dn = (gy > 0, gy < ny - 1)
    has_lf, has_rt = (gz > 0, gz < nz - 1)
    to_a, to_b = ({"view": va}, {"view": vb})
    to_up, to_dn = ({"gy": jnp.maximum(gy - 1, 0)}, {"gy": jnp.minimum(gy + 1, ny - 1)})
    to_lf, to_rt = ({"gz": jnp.maximum(gz - 1, 0)}, {"gz": jnp.minimum(gz + 1, nz - 1)})
    view_total = views * 4

    def mine(o):
        return pl.ds(o * own, own)

    def rcopy(src, dst, it, sid, dev):
        return pltpu.make_async_remote_copy(
            src_ref=src, dst_ref=dst, send_sem=ssem.at[it, sid], recv_sem=rsem.at[it, sid],
            device_id=dev, device_id_type=MESH,
        )

    def landed(dst, it, sid, dev):
        rcopy(dst, dst, it, sid, dev).wait_recv()

    def sent(src, it, sid, dev):
        rcopy(src, src, it, sid, dev).wait_send()

    for ref in (wl, wr, zl, zr, yu, yd, zp):
        ref[...] = jnp.zeros_like(ref)
    for e in (0, nb + 1):
        fg[e] = jnp.zeros((planes, hw, rows_z), F32)
    for vv in range(views):
        for e in (0, 1, nb + 2, nb + 3):
            gp[vv, e * blk : (e + 1) * blk, :] = jnp.zeros((blk, rows_z + LANES), BF)
    for b in range(nb):
        for p in range(own):
            fg[1 + b, own * v + p] = est[p, b * hw : (b + 1) * hw, :]

    barrier = pltpu.get_barrier_semaphore()
    for dev in (to_a, to_b):
        pl.semaphore_signal(barrier, inc=1, device_id=dev, device_id_type=MESH)
    for cond, dev in ((has_up, to_up), (has_dn, to_dn), (has_lf, to_lf), (has_rt, to_rt)):
        @pl.when(cond)
        def _():
            pl.semaphore_signal(barrier, inc=1, device_id=dev, device_id_type=MESH)
    sides = [c.astype(jnp.int32) for c in (has_up, has_dn, has_lf, has_rt)]
    pl.semaphore_wait(barrier, 2 + sides[0] + sides[1] + sides[2] + sides[3])

    s_p = 3 * ne
    s_yu, s_yd, s_zl, s_zr = (3 * ne + 3, 3 * ne + 4, 3 * ne + 5, 3 * ne + 6)
    s_r1 = 3 * ne + 7
    s_r2 = s_r1 + 2 * ne
    s_z = s_r2 + ne
    s_rl, s_rr, s_ru, s_rd = (s_z + 3, s_z + 4, s_z + 5, s_z + 6)

    def when_edge(e, fn):
        if e == 0:
            pl.when(has_up)(fn)
        elif e == nb + 1:
            pl.when(has_dn)(fn)
        else:
            fn()

    lane_h = lane_iota(hw)
    group_h = lane_h // (2 * hw)
    side_h = (lane_h // hw) % 2

    for it in range(ITERS):
        own_sl = mine(v)

        def ag_start(e):
            rcopy(fg.at[e, own_sl], fg.at[e, own_sl], it, ne + e, to_b).start()
            rcopy(fg.at[e, own_sl], fg.at[e, own_sl], it, e, to_a).start()

        def ag_forward(e):
            landed(fg.at[e, mine(vb)], it, ne + e, to_b)
            rcopy(fg.at[e, mine(vb)], fg.at[e, mine(vb)], it, 2 * ne + e, to_a).start()

        @pl.when(has_dn)
        def _():
            rcopy(fg.at[nb, own_sl], fg.at[0, own_sl], it, s_yd, to_dn).start()

        @pl.when(has_up)
        def _():
            rcopy(fg.at[1, own_sl], fg.at[nb + 1, own_sl], it, s_yu, to_up).start()

        for b in range(nb):
            ag_start(1 + b)

        if it == 0:
            for vv in range(views):
                build_depth(mt, vv, taps[0, 3 * vv + 2 : 3 * vv + 3, :], rows_z, hw)
                build_plane_row(
                    am, vv * blk, taps[0, 3 * vv : 3 * vv + 1, :],
                    taps[0, 3 * vv + 1 : 3 * vv + 2, :], planes, hw,
                )

        @pl.when(has_up)
        def _():
            landed(fg.at[0, own_sl], it, s_yd, to_up)
            ag_start(0)

        @pl.when(has_dn)
        def _():
            landed(fg.at[nb + 1, own_sl], it, s_yu, to_dn)
            ag_start(nb + 1)

        for e in range(ne):
            packed = jnp.zeros((hw, LANES), F32)
            for p in range(own):
                body = fg[e, own * v + p]
                first = roll_lanes(body[:, :LANES], 2 * hw * p + hw)
                last = roll_lanes(body[:, rows_z - LANES :], 2 * hw * p + hw)
                pair = jnp.where(side_h == 0, last, first)
                packed = jnp.where(group_h == p, pair, packed)
            wk[e] = packed

        @pl.when(has_lf)
        def _():
            rcopy(wk, wr, it, s_zl, to_lf).start()

        @pl.when(has_rt)
        def _():
            rcopy(wk, wl, it, s_zr, to_rt).start()

        ag_forward(1)

        if it == 0:
            for vv in range(views):
                build_plane_row(
                    bm.at[vv], 0, taps[1, 3 * vv : 3 * vv + 1, :],
                    taps[1, 3 * vv + 1 : 3 * vv + 2, :], planes, hw,
                )

        @pl.when(has_lf)
        def _():
            landed(wl, it, s_zr, to_lf)

        @pl.when(has_rt)
        def _():
            landed(wr, it, s_zl, to_rt)

        for e in range(ne):
            pk[v, e] = jnp.where(side_h == 0, wl[e], wr[e])
        rcopy(pk.at[v], pk.at[v], it, s_p + 1, to_b).start()
        rcopy(pk.at[v], pk.at[v], it, s_p, to_a).start()

        for b in range(1, nb):
            ag_forward(1 + b)
        for e in (0, nb + 1):
            when_edge(e, functools.partial(ag_forward, e))
        landed(pk.at[vb], it, s_p + 1, to_b)
        rcopy(pk.at[vb], pk.at[vb], it, s_p + 2, to_a).start()

        for e in range(ne):
            def arrivals(e=e):
                landed(fg.at[e, mine(va)], it, e, to_a)
                landed(fg.at[e, mine(vc)], it, 2 * ne + e, to_a)
            when_edge(e, arrivals)
        landed(pk.at[va], it, s_p, to_a)
        landed(pk.at[vc], it, s_p + 2, to_a)

        @pl.loop(0, ne)
        def _(e):
            base = pl.multiple_of(e * blk, blk)
            fb[pl.ds(base, blk), :rows_z] = fg[e].reshape(blk, rows_z).astype(BF)
            for x in range(planes):
                rim = jnp.where(group_h == x % own, pk[x // own, e], 0.0)
                fb[pl.ds(base + x * hw, hw), rows_z:] = rim.astype(BF)

        @pl.loop(0, nb)
        def _(b):
            base = pl.multiple_of(b * blk, blk)
            g = jnp.dot(am[...], fb[pl.ds(base, 3 * blk), :], preferred_element_type=F32).astype(BF)
            z_block = lax.broadcasted_iota(jnp.int32, (1, rows_z), 1) // BZ
            y_block = b * hw // BY
            for vv in range(views):
                scale = jnp.zeros((1, rows_z), F32)
                valid = jnp.zeros((1, rows_z), jnp.int32)
                for c in range(rows_z // BZ):
                    scale = jnp.where(z_block == c, scales[vv, y_block, c], scale)
                    valid = jnp.where(z_block == c, flags[vv, y_block, c], valid)
                blurred = lax.dot_general(
                    g[vv * blk : (vv + 1) * blk], mt[vv], (((1,), (1,)), ((), ())),
                    preferred_element_type=F32,
                )
                data = vd[vv, :, pl.ds(pl.multiple_of(b * hw, hw), hw), :].astype(F32)
                ratio = jnp.where(valid == 1, data.reshape(blk, rows_z) * scale / blurred, 1.0)
                spread = jnp.dot(ratio.astype(BF), mt[vv], preferred_element_type=F32)
                gp[vv, pl.ds(base + 2 * blk, blk), :] = spread.astype(BF)

        @pl.when(has_dn)
        def _():
            sent(fg.at[nb, own_sl], it, s_yd, to_dn)

        @pl.when(has_up)
        def _():
            sent(fg.at[1, own_sl], it, s_yu, to_up)

        @pl.when(has_lf)
        def _():
            sent(wk, it, s_zl, to_lf)

        @pl.when(has_rt)
        def _():
            sent(wk, it, s_zr, to_rt)

        for e in range(ne):
            def sends(e=e):
                sent(fg.at[e, own_sl], it, e, to_a)
                sent(fg.at[e, own_sl], it, ne + e, to_b)
                sent(fg.at[e, mine(vb)], it, 2 * ne + e, to_a)
            when_edge(e, sends)
        sent(pk.at[v], it, s_p, to_a)
        sent(pk.at[v], it, s_p + 1, to_b)
        sent(pk.at[vb], it, s_p + 2, to_a)

        def used(e):
            return ((e > 0) | has_up) & ((e < nb + 1) | has_dn)

        def r1_copy(e, k):
            owner = (va, vc)[k]
            return rcopy(ob.at[e, mine(owner)], r1.at[e, k], it, s_r1 + 2 * e + k, to_a)

        @pl.loop(0, ne)
        def _(e):
            @pl.when(used(e))
            def _():
                rows = pl.ds(pl.multiple_of(e * blk, blk), 3 * blk)
                total = jnp.dot(bm[0], gp[0, rows, :], preferred_element_type=F32)
                for vv in range(1, views):
                    total = total + jnp.dot(bm[vv], gp[vv, rows, :], preferred_element_type=F32)
                ob[e] = total[:, :rows_z].reshape(planes, hw, rows_z)
                r1_copy(e, 1).start()
                r1_copy(e, 0).start()
                rims = total[:, rows_z:].reshape(planes, hw, LANES)
                for o in range(planes // own):
                    packed = rims[own * o]
                    for p in range(1, own):
                        packed = jnp.where(group_h == p, rims[own * o + p], packed)
                    zp[o, e] = packed

        rcopy(zp.at[vc], r1z.at[1], it, s_z + 1, to_a).start()
        rcopy(zp.at[va], r1z.at[0], it, s_z, to_a).start()

        @pl.loop(0, ne)
        def _(e):
            @pl.when(used(e))
            def _():
                r1_copy(e, 1).wait_recv()
                s2[e] = ob[e, mine(vb)] + r1[e, 1]
                rcopy(s2.at[e], r2.at[e], it, s_r2 + e, to_b).start()

        landed(r1z.at[1], it, s_z + 1, to_a)
        s2z[...] = zp[vb] + r1z[1]
        rcopy(s2z, r2z, it, s_z + 2, to_b).start()

        @pl.loop(0, ne)
        def _(e):
            @pl.when(used(e))
            def _():
                r1_copy(e, 0).wait_recv()
                landed(r2.at[e], it, s_r2 + e, to_b)
                ub[e] = ob[e, own_sl] + r1[e, 0] + r2[e]

        landed(r1z.at[0], it, s_z, to_a)
        landed(r2z, it, s_z + 2, to_b)
        zu[...] = zp[v] + r1z[0] + r2z[...]

        @pl.when(has_lf)
        def _():
            rcopy(zu, zr, it, s_rl, to_lf).start()

        @pl.when(has_rt)
        def _():
            rcopy(zu, zl, it, s_rr, to_rt).start()

        @pl.when(has_rt)
        def _():
            landed(zr, it, s_rl, to_rt)

        @pl.when(has_lf)
        def _():
            landed(zl, it, s_rr, to_lf)

        for e in range(ne):
            def add_rims(e=e):
                for p in range(own):
                    last = roll_lanes(zr[e], LANES - hw - 2 * hw * p)
                    first = roll_lanes(zl[e], -(2 * hw * p + hw))
                    ub[e, p, :, :LANES] += jnp.where(lane_h < hw, first, 0.0)
                    ub[e, p, :, rows_z - LANES :] += jnp.where(lane_h >= LANES - hw, last, 0.0)
            when_edge(e, add_rims)

        @pl.when(has_up)
        def _():
            rcopy(ub.at[0], yd, it, s_ru, to_up).start()

        @pl.when(has_dn)
        def _():
            rcopy(ub.at[nb + 1], yu, it, s_rd, to_dn).start()

        @pl.when(has_dn)
        def _():
            landed(yd, it, s_ru, to_dn)

        @pl.when(has_up)
        def _():
            landed(yu, it, s_rd, to_up)

        for b in range(nb):
            for p in range(own):
                total = ub[1 + b, p]
                if b == 0:
                    total = total + yu[p]
                if b == nb - 1:
                    total = total + yd[p]
                fresh = fg[1 + b, own * v + p] * total / view_total
                if it + 1 < ITERS:
                    fg[1 + b, own * v + p] = fresh
                else:
                    out[p, b * hw : (b + 1) * hw, :] = fresh

        @pl.loop(0, ne)
        def _(e):
            @pl.when(used(e))
            def _():
                r1_copy(e, 0).wait_send()
                r1_copy(e, 1).wait_send()
                sent(s2.at[e], it, s_r2 + e, to_b)

        sent(zp.at[va], it, s_z, to_a)
        sent(zp.at[vc], it, s_z + 1, to_a)
        sent(s2z, it, s_z + 2, to_b)

        @pl.when(has_lf)
        def _():
            sent(zu, it, s_rl, to_lf)

        @pl.when(has_rt)
        def _():
            sent(zu, it, s_rr, to_rt)

        @pl.when(has_up)
        def _():
            sent(ub.at[0], it, s_ru, to_up)

        @pl.when(has_dn)
        def _():
            sent(ub.at[nb + 1], it, s_rd, to_dn)


def per_device(ny, nz, estimate, view_data, block_scales, block_flags, profile, supports):
    views, planes, rows_y, rows_z = view_data.shape
    own = estimate.shape[0]
    hw = (profile.shape[2] - 1) // 2
    nb = rows_y // hw
    ne = nb + 2
    blk = planes * hw
    wide = rows_z + LANES
    forward = kernel_table(profile, supports)
    both = jnp.stack([forward, forward[:, :, ::-1]]).reshape(2, views * 3, profile.shape[2])
    taps = jnp.pad(both, ((0, 0), (0, 0), (0, LANES - profile.shape[2])))
    owners = planes // own
    n_sem = 6 * ne + 7 + 7
    vm = pltpu.VMEM
    scratch = [
        vm((ne, planes, hw, rows_z), F32),
        vm((owners, ne, hw, LANES), F32),
        vm((ne, hw, LANES), F32),
        vm((ne, hw, LANES), F32),
        vm((ne, hw, LANES), F32),
        vm((ne * blk, wide), BF),
        vm((views * blk, 3 * blk), BF),
        vm((views, blk, 3 * blk), BF),
        vm((views, rows_z, wide), BF),
        vm((views, (nb + 4) * blk, wide), BF),
        vm((ne, planes, hw, rows_z), F32),
        vm((owners, ne, hw, LANES), F32),
        vm((ne, 2, own, hw, rows_z), F32),
        vm((2, ne, hw, LANES), F32),
        vm((ne, own, hw, rows_z), F32),
        vm((ne, hw, LANES), F32),
        vm((ne, own, hw, rows_z), F32),
        vm((ne, hw, LANES), F32),
        vm((ne, own, hw, rows_z), F32),
        vm((ne, hw, LANES), F32),
        vm((ne, hw, LANES), F32),
        vm((ne, hw, LANES), F32),
        vm((own, hw, rows_z), F32),
        vm((own, hw, rows_z), F32),
        pltpu.SemaphoreType.DMA((ITERS, n_sem)),
        pltpu.SemaphoreType.DMA((ITERS, n_sem)),
    ]
    in_vm = pl.BlockSpec(memory_space=pltpu.VMEM)
    in_sm = pl.BlockSpec(memory_space=pltpu.SMEM)
    return pl.pallas_call(
        functools.partial(kernel, (ny, nz, views, planes, rows_y, rows_z, own, hw)),
        out_shape=jax.ShapeDtypeStruct(estimate.shape, F32),
        in_specs=[in_vm, in_vm, in_sm, in_sm, in_vm],
        out_specs=in_vm,
        scratch_shapes=scratch,
        compiler_params=pltpu.CompilerParams(collective_id=0, has_side_effects=True),
    )(estimate, view_data, block_scales, block_flags, taps)


def solution(mesh):
    placed = (
        P("view", "gy", "gz"),
        P("view", None, "gy", "gz"),
        P("view", "gy", "gz"),
        P("view", "gy", "gz"),
        P("view", None, None),
        P("view", None),
    )
    body = functools.partial(per_device, mesh.shape["gy"], mesh.shape["gz"])
    return jax.shard_map(
        body, mesh=mesh, in_specs=placed, out_specs=P("view", "gy", "gz"), check_vma=False
    )
```

```python
import functools

import jax
import jax.numpy as jnp
from jax import lax
from jax.experimental import pallas as pl
from jax.experimental.pallas import tpu as pltpu
from jax.sharding import PartitionSpec as P

BY = 32
BZ = 64
ITERS = 2
LANES = 128
MESH = pl.DeviceIdType.MESH
BF = jnp.bfloat16
F32 = jnp.float32


def kernel_table(profile, supports):
    tap_count = profile.shape[-1]
    distance = jnp.abs(jnp.arange(tap_count, dtype=jnp.int32) - (tap_count - 1) // 2)
    inside = distance[None, None, :] <= supports[:, :, None]
    masked = jnp.where(inside, profile, 0.0)
    return masked / jnp.sum(masked, axis=-1, keepdims=True)


def lane_iota(rows):
    return lax.broadcasted_iota(jnp.int32, (rows, LANES), 1)


def toeplitz(row, rows, shift):
    wide = jnp.broadcast_to(row, (rows, LANES))
    return pltpu.roll(wide, shift % LANES, 1, stride=1, stride_axis=0)


def roll_lanes(x, shift):
    shift = shift % LANES
    return pltpu.roll(x, shift, 1) if shift else x


def build_plane_row(dst, row_base, kx, ky, planes, hw):
    lane = lane_iota(hw)
    per_tile = LANES // hw
    halves = planes // per_tile
    tall = toeplitz(ky, hw, 0)
    bands = []
    for d in range(3):
        q = jnp.where(lane < hw, roll_lanes(tall, -hw * d), 0.0)
        width = hw
        while width < LANES:
            q = q + roll_lanes(q, width)
            width *= 2
        bands.append(q)
    tx = toeplitz(kx, planes, -hw)
    row_id = lax.broadcasted_iota(jnp.int32, (LANES, LANES), 0)
    group = lax.broadcasted_iota(jnp.int32, (LANES, LANES), 1) // hw
    for half in range(halves):
        pick = (row_id == group + half * per_tile).astype(F32)
        spread = jnp.dot(tx, pick, precision=lax.Precision.HIGHEST, preferred_element_type=F32)
        for d in range(3):
            for x in range(planes):
                tile = spread[x : x + 1, :] * bands[d]
                c0 = (halves * d + half) * LANES
                dst[row_base + x * hw : row_base + (x + 1) * hw, c0 : c0 + LANES] = tile.astype(BF)


def build_depth(dst, v, kz, rows_z, hw):
    row_j = lax.broadcasted_iota(jnp.int32, (rows_z, LANES), 0)
    lane = lane_iota(rows_z)
    reps = rows_z // LANES
    t = jnp.concatenate([toeplitz(kz, LANES, -hw)] * reps, axis=0)
    for ct in range(reps):
        c = lane + ct * LANES
        keep = jnp.abs(c - row_j) <= hw
        dst[v, :, ct * LANES : (ct + 1) * LANES] = jnp.where(keep, t, 0.0).astype(BF)
    h = jnp.concatenate([toeplitz(kz, LANES, 0)] * reps, axis=0)
    low = (row_j < hw) & (lane < hw)
    high = (row_j >= rows_z - hw) & (lane >= hw) & (lane < 2 * hw)
    h = jnp.where(low | high, h, 0.0)
    width = 2 * hw
    while width < LANES:
        h = h + roll_lanes(h, width)
        width *= 2
    dst[v, :, rows_z : rows_z + LANES] = h.astype(BF)


def kernel(
    sizes, est, vd_any, scales, flags, taps, out,
    fg, pk, wk, wl, wr, fb, am, bm, mt, gp, ob, zp,
    r1, r1z, s2, s2z, r2, r2z, ub, zu, zl, zr, yu, yd, vd, dsem, ssem, rsem,
):
    ny, nz, views, planes, rows_y, rows_z, own, hw = sizes
    nb = rows_y // hw
    ne = nb + 2
    blk = planes * hw
    v = lax.axis_index("view")
    gy = lax.axis_index("gy")
    gz = lax.axis_index("gz")
    va, vb, vc = (lax.bitwise_xor(v, 1), lax.bitwise_xor(v, 2), lax.bitwise_xor(v, 3))
    has_up, has_dn = (gy > 0, gy < ny - 1)
    has_lf, has_rt = (gz > 0, gz < nz - 1)
    to_a, to_b = ({"view": va}, {"view": vb})
    to_up, to_dn = ({"gy": jnp.maximum(gy - 1, 0)}, {"gy": jnp.minimum(gy + 1, ny - 1)})
    to_lf, to_rt = ({"gz": jnp.maximum(gz - 1, 0)}, {"gz": jnp.minimum(gz + 1, nz - 1)})
    view_total = views * 4

    def mine(o):
        return pl.ds(o * own, own)

    def rcopy(src, dst, it, sid, dev):
        return pltpu.make_async_remote_copy(
            src_ref=src, dst_ref=dst, send_sem=ssem.at[it, sid], recv_sem=rsem.at[it, sid],
            device_id=dev, device_id_type=MESH,
        )

    def landed(dst, it, sid, dev):
        rcopy(dst, dst, it, sid, dev).wait_recv()

    def sent(src, it, sid, dev):
        rcopy(src, src, it, sid, dev).wait_send()

    load = pltpu.make_async_copy(vd_any, vd, dsem)
    load.start()
    for ref in (wl, wr, zl, zr, yu, yd, zp):
        ref[...] = jnp.zeros_like(ref)
    for e in (0, nb + 1):
        fg[e] = jnp.zeros((planes, hw, rows_z), F32)
    for vv in range(views):
        for e in (0, 1, nb + 2, nb + 3):
            gp[vv, e * blk : (e + 1) * blk, :] = jnp.zeros((blk, rows_z + LANES), BF)
    for b in range(nb):
        for p in range(own):
            fg[1 + b, own * v + p] = est[p, b * hw : (b + 1) * hw, :]

    barrier = pltpu.get_barrier_semaphore()
    for dev in (to_a, to_b):
        pl.semaphore_signal(barrier, inc=1, device_id=dev, device_id_type=MESH)
    for cond, dev in ((has_up, to_up), (has_dn, to_dn), (has_lf, to_lf), (has_rt, to_rt)):
        @pl.when(cond)
        def _():
            pl.semaphore_signal(barrier, inc=1, device_id=dev, device_id_type=MESH)
    sides = [c.astype(jnp.int32) for c in (has_up, has_dn, has_lf, has_rt)]
    pl.semaphore_wait(barrier, 2 + sides[0] + sides[1] + sides[2] + sides[3])

    s_p = 3 * ne
    s_yu, s_yd, s_zl, s_zr = (3 * ne + 3, 3 * ne + 4, 3 * ne + 5, 3 * ne + 6)
    s_r1 = 3 * ne + 7
    s_r2 = s_r1 + 2 * ne
    s_z = s_r2 + ne
    s_rl, s_rr, s_ru, s_rd = (s_z + 3, s_z + 4, s_z + 5, s_z + 6)

    def when_edge(e, fn):
        if e == 0:
            pl.when(has_up)(fn)
        elif e == nb + 1:
            pl.when(has_dn)(fn)
        else:
            fn()

    lane_h = lane_iota(hw)
    group_h = lane_h // (2 * hw)
    side_h = (lane_h // hw) % 2

    blocks = list(range(2, nb)) + [1, nb]
    order = blocks + [0, nb + 1]
    own_sl = mine(v)
    gains = []

    def ag_start(it, e):
        rcopy(fg.at[e, own_sl], fg.at[e, own_sl], it, ne + e, to_b).start()
        rcopy(fg.at[e, own_sl], fg.at[e, own_sl], it, e, to_a).start()

    def rims_start(it):
        @pl.when(has_dn)
        def _():
            rcopy(fg.at[nb, own_sl], fg.at[0, own_sl], it, s_yd, to_dn).start()

        @pl.when(has_up)
        def _():
            rcopy(fg.at[1, own_sl], fg.at[nb + 1, own_sl], it, s_yu, to_up).start()

    rims_start(0)
    for e in blocks:
        ag_start(0, e)

    for it in range(ITERS):

        def ag_forward(e):
            landed(fg.at[e, mine(vb)], it, ne + e, to_b)
            rcopy(fg.at[e, mine(vb)], fg.at[e, mine(vb)], it, 2 * ne + e, to_a).start()

        if it == 0:
            for vv in range(views):
                build_depth(mt, vv, taps[0, 3 * vv + 2 : 3 * vv + 3, :], rows_z, hw)
                build_plane_row(
                    am, vv * blk, taps[0, 3 * vv : 3 * vv + 1, :],
                    taps[0, 3 * vv + 1 : 3 * vv + 2, :], planes, hw,
                )

        @pl.when(has_up)
        def _():
            landed(fg.at[0, own_sl], it, s_yd, to_up)
            ag_start(it, 0)

        @pl.when(has_dn)
        def _():
            landed(fg.at[nb + 1, own_sl], it, s_yu, to_dn)
            ag_start(it, nb + 1)

        for e in range(ne):
            packed = jnp.zeros((hw, LANES), F32)
            for p in range(own):
                body = fg[e, own * v + p]
                first = roll_lanes(body[:, :LANES], 2 * hw * p + hw)
                last = roll_lanes(body[:, rows_z - LANES :], 2 * hw * p + hw)
                pair = jnp.where(side_h == 0, last, first)
                packed = jnp.where(group_h == p, pair, packed)
            wk[e] = packed

        @pl.when(has_lf)
        def _():
            rcopy(wk, wr, it, s_zl, to_lf).start()

        @pl.when(has_rt)
        def _():
            rcopy(wk, wl, it, s_zr, to_rt).start()

        ag_forward(blocks[0])

        if it == 0:
            for vv in range(views):
                build_plane_row(
                    bm.at[vv], 0, taps[1, 3 * vv : 3 * vv + 1, :],
                    taps[1, 3 * vv + 1 : 3 * vv + 2, :], planes, hw,
                )
            for vv in range(views):
                mid = planes // 2 * hw
                along_z = mt[vv, rows_z // 2 : rows_z // 2 + 1, :rows_z].astype(F32)
                along_z = jnp.sum(along_z, axis=1, keepdims=True)
                fwd = am[vv * blk + mid : vv * blk + mid + 1, :].astype(F32)
                bwd = bm[vv, mid : mid + 1, :].astype(F32)
                gains.append((
                    jnp.sum(fwd, axis=1, keepdims=True) * along_z,
                    1.0 / (jnp.sum(bwd, axis=1, keepdims=True) * along_z),
                ))
            load.wait()

        @pl.when(has_lf)
        def _():
            landed(wl, it, s_zr, to_lf)

        @pl.when(has_rt)
        def _():
            landed(wr, it, s_zl, to_rt)

        for e in range(ne):
            pk[v, e] = jnp.where(side_h == 0, wl[e], wr[e])
        rcopy(pk.at[v], pk.at[v], it, s_p + 1, to_b).start()
        rcopy(pk.at[v], pk.at[v], it, s_p, to_a).start()

        for e in blocks[1:]:
            ag_forward(e)
        for e in (0, nb + 1):
            when_edge(e, functools.partial(ag_forward, e))
        landed(pk.at[vb], it, s_p + 1, to_b)
        rcopy(pk.at[vb], pk.at[vb], it, s_p + 2, to_a).start()

        for e in order:
            def arrivals(e=e):
                landed(fg.at[e, mine(va)], it, e, to_a)
                landed(fg.at[e, mine(vc)], it, 2 * ne + e, to_a)
            when_edge(e, arrivals)
            fb[e * blk : (e + 1) * blk, :rows_z] = fg[e].reshape(blk, rows_z).astype(BF)
        landed(pk.at[va], it, s_p, to_a)
        landed(pk.at[vc], it, s_p + 2, to_a)

        @pl.loop(0, ne)
        def _(e):
            base = pl.multiple_of(e * blk, blk)
            for x in range(planes):
                rim = jnp.where(group_h == x % own, pk[x // own, e], 0.0)
                fb[pl.ds(base + x * hw, hw), rows_z:] = rim.astype(BF)

        @pl.loop(0, nb)
        def _(b):
            base = pl.multiple_of(b * blk, blk)
            g = jnp.dot(am[...], fb[pl.ds(base, 3 * blk), :], preferred_element_type=F32).astype(BF)
            z_block = lax.broadcasted_iota(jnp.int32, (1, rows_z), 1) // BZ
            y_block = b * hw // BY
            for vv in range(views):
                scale = jnp.zeros((1, rows_z), F32)
                valid = jnp.zeros((1, rows_z), jnp.int32)
                for c in range(rows_z // BZ):
                    scale = jnp.where(z_block == c, scales[vv, y_block, c], scale)
                    valid = jnp.where(z_block == c, flags[vv, y_block, c], valid)
                blurred = lax.dot_general(
                    g[vv * blk : (vv + 1) * blk], mt[vv], (((1,), (1,)), ((), ())),
                    preferred_element_type=F32,
                )
                data = vd[vv, :, pl.ds(pl.multiple_of(b * hw, hw), hw), :].astype(F32)
                ratio = jnp.where(
                    valid == 1, data.reshape(blk, rows_z) * (scale * gains[vv][0]) / blurred, 1.0
                )
                spread = jnp.dot((ratio * gains[vv][1]).astype(BF), mt[vv], preferred_element_type=F32)
                gp[vv, pl.ds(base + 2 * blk, blk), :] = spread.astype(BF)

        @pl.when(has_dn)
        def _():
            sent(fg.at[nb, own_sl], it, s_yd, to_dn)

        @pl.when(has_up)
        def _():
            sent(fg.at[1, own_sl], it, s_yu, to_up)

        @pl.when(has_lf)
        def _():
            sent(wk, it, s_zl, to_lf)

        @pl.when(has_rt)
        def _():
            sent(wk, it, s_zr, to_rt)

        for e in range(ne):
            def sends(e=e):
                sent(fg.at[e, own_sl], it, e, to_a)
                sent(fg.at[e, own_sl], it, ne + e, to_b)
                sent(fg.at[e, mine(vb)], it, 2 * ne + e, to_a)
            when_edge(e, sends)
        sent(pk.at[v], it, s_p, to_a)
        sent(pk.at[v], it, s_p + 1, to_b)
        sent(pk.at[vb], it, s_p + 2, to_a)

        def used(e):
            return ((e > 0) | has_up) & ((e < nb + 1) | has_dn)

        def r1_copy(e, k):
            owner = (va, vc)[k]
            return rcopy(ob.at[e, mine(owner)], r1.at[e, k], it, s_r1 + 2 * e + k, to_a)

        def back(e, lanes):
            rows = pl.ds(pl.multiple_of(e * blk, blk), 3 * blk)
            total = jnp.dot(bm[0], gp[0, rows, lanes], preferred_element_type=F32)
            for vv in range(1, views):
                total = total + jnp.dot(bm[vv], gp[vv, rows, lanes], preferred_element_type=F32)
            return total

        @pl.loop(0, ne)
        def _(e):
            @pl.when(used(e))
            def _():
                rims = back(e, slice(rows_z, None)).reshape(planes, hw, LANES)
                for o in range(planes // own):
                    packed = rims[own * o]
                    for p in range(1, own):
                        packed = jnp.where(group_h == p, rims[own * o + p], packed)
                    zp[o, e] = packed

        rcopy(zp.at[vc], r1z.at[1], it, s_z + 1, to_a).start()
        rcopy(zp.at[va], r1z.at[0], it, s_z, to_a).start()

        def nth(i):
            e = jnp.where(i == nb, 1, jnp.where(i == nb + 1, nb, i))
            return jnp.where(i == 0, 0, jnp.where(i == 1, nb + 1, e))

        @pl.loop(0, ne + 1)
        def _(i):
            e = nth(i)
            @pl.when((i < ne) & used(e))
            def _():
                ob[e] = back(e, slice(0, rows_z)).reshape(planes, hw, rows_z)
                r1_copy(e, 1).start()
                r1_copy(e, 0).start()

            @pl.when(i == 1)
            def _():
                landed(r1z.at[1], it, s_z + 1, to_a)
                s2z[...] = zp[vb] + r1z[1]
                rcopy(s2z, r2z, it, s_z + 2, to_b).start()

            q = nth(jnp.maximum(i - 1, 0))
            @pl.when((i > 0) & used(q))
            def _():
                r1_copy(q, 1).wait_recv()
                s2[q] = ob[q, mine(vb)] + r1[q, 1]
                rcopy(s2.at[q], r2.at[q], it, s_r2 + q, to_b).start()

        landed(r1z.at[0], it, s_z, to_a)
        landed(r2z, it, s_z + 2, to_b)
        zu[...] = zp[v] + r1z[0] + r2z[...]

        @pl.when(has_lf)
        def _():
            rcopy(zu, zr, it, s_rl, to_lf).start()

        @pl.when(has_rt)
        def _():
            rcopy(zu, zl, it, s_rr, to_rt).start()

        def gather_sum(e):
            r1_copy(e, 0).wait_recv()
            landed(r2.at[e], it, s_r2 + e, to_b)
            ub[e] = ob[e, own_sl] + r1[e, 0] + r2[e]

        def add_rims(e):
            for p in range(own):
                last = roll_lanes(zr[e], LANES - hw - 2 * hw * p)
                first = roll_lanes(zl[e], -(2 * hw * p + hw))
                ub[e, p, :, :LANES] += jnp.where(lane_h < hw, first, 0.0)
                ub[e, p, :, rows_z - LANES :] += jnp.where(lane_h >= LANES - hw, last, 0.0)

        for e in (0, nb + 1):
            when_edge(e, functools.partial(gather_sum, e))

        @pl.when(has_rt)
        def _():
            landed(zr, it, s_rl, to_rt)

        @pl.when(has_lf)
        def _():
            landed(zl, it, s_rr, to_lf)

        for e in (0, nb + 1):
            when_edge(e, functools.partial(add_rims, e))

        @pl.when(has_up)
        def _():
            rcopy(ub.at[0], yd, it, s_ru, to_up).start()

        @pl.when(has_dn)
        def _():
            rcopy(ub.at[nb + 1], yu, it, s_rd, to_dn).start()

        for e in blocks:
            gather_sum(e)
            add_rims(e)
            if e == 1:
                @pl.when(has_up)
                def _():
                    landed(yu, it, s_rd, to_up)
            if e == nb:
                @pl.when(has_dn)
                def _():
                    landed(yd, it, s_ru, to_dn)
            for p in range(own):
                total = ub[e, p]
                if e == 1:
                    total = total + yu[p]
                if e == nb:
                    total = total + yd[p]
                fresh = fg[e, own * v + p] * total / view_total
                if it + 1 < ITERS:
                    fg[e, own * v + p] = fresh
                else:
                    out[p, (e - 1) * hw : e * hw, :] = fresh
            if it + 1 < ITERS:
                ag_start(it + 1, e)
        if it + 1 < ITERS:
            rims_start(it + 1)

        @pl.loop(0, ne)
        def _(e):
            @pl.when(used(e))
            def _():
                r1_copy(e, 0).wait_send()
                r1_copy(e, 1).wait_send()
                sent(s2.at[e], it, s_r2 + e, to_b)

        sent(zp.at[va], it, s_z, to_a)
        sent(zp.at[vc], it, s_z + 1, to_a)
        sent(s2z, it, s_z + 2, to_b)

        @pl.when(has_lf)
        def _():
            sent(zu, it, s_rl, to_lf)

        @pl.when(has_rt)
        def _():
            sent(zu, it, s_rr, to_rt)

        @pl.when(has_up)
        def _():
            sent(ub.at[0], it, s_ru, to_up)

        @pl.when(has_dn)
        def _():
            sent(ub.at[nb + 1], it, s_rd, to_dn)


def per_device(ny, nz, estimate, view_data, block_scales, block_flags, profile, supports):
    views, planes, rows_y, rows_z = view_data.shape
    own = estimate.shape[0]
    hw = (profile.shape[2] - 1) // 2
    nb = rows_y // hw
    ne = nb + 2
    blk = planes * hw
    wide = rows_z + LANES
    forward = kernel_table(profile, supports)
    both = jnp.stack([forward, forward[:, :, ::-1]]).reshape(2, views * 3, profile.shape[2])
    taps = jnp.pad(both, ((0, 0), (0, 0), (0, LANES - profile.shape[2])))
    owners = planes // own
    n_sem = 6 * ne + 7 + 7
    vm = pltpu.VMEM
    scratch = [
        vm((ne, planes, hw, rows_z), F32),
        vm((owners, ne, hw, LANES), F32),
        vm((ne, hw, LANES), F32),
        vm((ne, hw, LANES), F32),
        vm((ne, hw, LANES), F32),
        vm((ne * blk, wide), BF),
        vm((views * blk, 3 * blk), BF),
        vm((views, blk, 3 * blk), BF),
        vm((views, rows_z, wide), BF),
        vm((views, (nb + 4) * blk, wide), BF),
        vm((ne, planes, hw, rows_z), F32),
        vm((owners, ne, hw, LANES), F32),
        vm((ne, 2, own, hw, rows_z), F32),
        vm((2, ne, hw, LANES), F32),
        vm((ne, own, hw, rows_z), F32),
        vm((ne, hw, LANES), F32),
        vm((ne, own, hw, rows_z), F32),
        vm((ne, hw, LANES), F32),
        vm((ne, own, hw, rows_z), F32),
        vm((ne, hw, LANES), F32),
        vm((ne, hw, LANES), F32),
        vm((ne, hw, LANES), F32),
        vm((own, hw, rows_z), F32),
        vm((own, hw, rows_z), F32),
        vm(view_data.shape, view_data.dtype),
        pltpu.SemaphoreType.DMA,
        pltpu.SemaphoreType.DMA((ITERS, n_sem)),
        pltpu.SemaphoreType.DMA((ITERS, n_sem)),
    ]
    in_vm = pl.BlockSpec(memory_space=pltpu.VMEM)
    in_sm = pl.BlockSpec(memory_space=pltpu.SMEM)
    return pl.pallas_call(
        functools.partial(kernel, (ny, nz, views, planes, rows_y, rows_z, own, hw)),
        out_shape=jax.ShapeDtypeStruct(estimate.shape, F32),
        in_specs=[in_vm, pl.BlockSpec(memory_space=pl.ANY), in_sm, in_sm, in_vm],
        out_specs=in_vm,
        scratch_shapes=scratch,
        compiler_params=pltpu.CompilerParams(collective_id=0, has_side_effects=True),
    )(estimate, view_data, block_scales, block_flags, taps)


def solution(mesh):
    placed = (
        P("view", "gy", "gz"),
        P("view", None, "gy", "gz"),
        P("view", "gy", "gz"),
        P("view", "gy", "gz"),
        P("view", None, None),
        P("view", None),
    )
    body = functools.partial(per_device, mesh.shape["gy"], mesh.shape["gz"])
    return jax.shard_map(
        body, mesh=mesh, in_specs=placed, out_specs=P("view", "gy", "gz"), check_vma=False
    )
```

```python
import functools

import jax
import jax.numpy as jnp
from jax import lax
from jax.experimental import pallas as pl
from jax.experimental.pallas import tpu as pltpu
from jax.sharding import PartitionSpec as P

BY = 32
BZ = 64
ITERS = 2
LANES = 128
MESH = pl.DeviceIdType.MESH
BF = jnp.bfloat16
F32 = jnp.float32


def kernel_table(profile, supports):
    tap_count = profile.shape[-1]
    distance = jnp.abs(jnp.arange(tap_count, dtype=jnp.int32) - (tap_count - 1) // 2)
    inside = distance[None, None, :] <= supports[:, :, None]
    masked = jnp.where(inside, profile, 0.0)
    return masked / jnp.sum(masked, axis=-1, keepdims=True)


def lane_iota(rows):
    return lax.broadcasted_iota(jnp.int32, (rows, LANES), 1)


def toeplitz(row, rows, shift):
    wide = jnp.broadcast_to(row, (rows, LANES))
    return pltpu.roll(wide, shift % LANES, 1, stride=1, stride_axis=0)


def roll_lanes(x, shift):
    shift = shift % LANES
    return pltpu.roll(x, shift, 1) if shift else x


def build_plane_row(dst, row_base, kx, ky, planes, hw):
    lane = lane_iota(hw)
    per_tile = LANES // hw
    halves = planes // per_tile
    tall = toeplitz(ky, hw, 0)
    bands = []
    for d in range(3):
        q = jnp.where(lane < hw, roll_lanes(tall, -hw * d), 0.0)
        width = hw
        while width < LANES:
            q = q + roll_lanes(q, width)
            width *= 2
        bands.append(q)
    tx = toeplitz(kx, planes, -hw)
    row_id = lax.broadcasted_iota(jnp.int32, (LANES, LANES), 0)
    group = lax.broadcasted_iota(jnp.int32, (LANES, LANES), 1) // hw
    for half in range(halves):
        pick = (row_id == group + half * per_tile).astype(F32)
        spread = jnp.dot(tx, pick, precision=lax.Precision.HIGHEST, preferred_element_type=F32)
        for d in range(3):
            for x in range(planes):
                tile = spread[x : x + 1, :] * bands[d]
                c0 = (halves * d + half) * LANES
                dst[row_base + x * hw : row_base + (x + 1) * hw, c0 : c0 + LANES] = tile.astype(BF)


def build_depth(dst, v, kz, rows_z, hw):
    row_j = lax.broadcasted_iota(jnp.int32, (rows_z, LANES), 0)
    lane = lane_iota(rows_z)
    reps = rows_z // LANES
    t = jnp.concatenate([toeplitz(kz, LANES, -hw)] * reps, axis=0)
    for ct in range(reps):
        c = lane + ct * LANES
        keep = jnp.abs(c - row_j) <= hw
        dst[v, :, ct * LANES : (ct + 1) * LANES] = jnp.where(keep, t, 0.0).astype(BF)
    h = jnp.concatenate([toeplitz(kz, LANES, 0)] * reps, axis=0)
    low = (row_j < hw) & (lane < hw)
    high = (row_j >= rows_z - hw) & (lane >= hw) & (lane < 2 * hw)
    h = jnp.where(low | high, h, 0.0)
    width = 2 * hw
    while width < LANES:
        h = h + roll_lanes(h, width)
        width *= 2
    dst[v, :, rows_z : rows_z + LANES] = h.astype(BF)


def kernel(
    sizes, est, vd_any, scales, flags, taps, out,
    fg, pk, wk, wl, wr, fb, am, bm, mt, gp, ob, zp,
    r1, r1z, s2, s2z, r2, r2z, ub, zu, zl, zr, yu, yd, vd, rb, g1, gs, dsem, ssem, rsem,
):
    ny, nz, views, planes, rows_y, rows_z, own, hw = sizes
    nb = rows_y // hw
    ne = nb + 2
    blk = planes * hw
    v = lax.axis_index("view")
    gy = lax.axis_index("gy")
    gz = lax.axis_index("gz")
    va, vb, vc = (lax.bitwise_xor(v, 1), lax.bitwise_xor(v, 2), lax.bitwise_xor(v, 3))
    has_up, has_dn = (gy > 0, gy < ny - 1)
    has_lf, has_rt = (gz > 0, gz < nz - 1)
    to_a, to_b = ({"view": va}, {"view": vb})
    to_up, to_dn = ({"gy": jnp.maximum(gy - 1, 0)}, {"gy": jnp.minimum(gy + 1, ny - 1)})
    to_lf, to_rt = ({"gz": jnp.maximum(gz - 1, 0)}, {"gz": jnp.minimum(gz + 1, nz - 1)})
    view_total = views * 4

    def mine(o):
        return pl.ds(o * own, own)

    def rcopy(src, dst, it, sid, dev):
        return pltpu.make_async_remote_copy(
            src_ref=src, dst_ref=dst, send_sem=ssem.at[it, sid], recv_sem=rsem.at[it, sid],
            device_id=dev, device_id_type=MESH,
        )

    def landed(dst, it, sid, dev):
        rcopy(dst, dst, it, sid, dev).wait_recv()

    def sent(src, it, sid, dev):
        rcopy(src, src, it, sid, dev).wait_send()

    load = pltpu.make_async_copy(vd_any, vd, dsem)
    load.start()
    for ref in (wl, wr, zl, zr, yu, yd, zp):
        ref[...] = jnp.zeros_like(ref)
    for e in (0, nb + 1):
        fg[e] = jnp.zeros((planes, hw, rows_z), F32)
    for vv in range(views):
        for e in (0, 1, nb + 2, nb + 3):
            gp[vv, e * blk : (e + 1) * blk, :] = jnp.zeros((blk, rows_z + LANES), BF)
    for b in range(nb):
        for p in range(own):
            fg[1 + b, own * v + p] = est[p, b * hw : (b + 1) * hw, :]

    barrier = pltpu.get_barrier_semaphore()
    for dev in (to_a, to_b):
        pl.semaphore_signal(barrier, inc=1, device_id=dev, device_id_type=MESH)
    for cond, dev in ((has_up, to_up), (has_dn, to_dn), (has_lf, to_lf), (has_rt, to_rt)):
        @pl.when(cond)
        def _():
            pl.semaphore_signal(barrier, inc=1, device_id=dev, device_id_type=MESH)
    sides = [c.astype(jnp.int32) for c in (has_up, has_dn, has_lf, has_rt)]
    pl.semaphore_wait(barrier, 2 + sides[0] + sides[1] + sides[2] + sides[3])

    s_p = 3 * ne
    s_yu, s_yd, s_zl, s_zr = (3 * ne + 3, 3 * ne + 4, 3 * ne + 5, 3 * ne + 6)
    s_r1 = 3 * ne + 7
    s_r2 = s_r1 + 2 * ne
    s_z = s_r2 + ne
    s_rl, s_rr, s_ru, s_rd = (s_z + 3, s_z + 4, s_z + 5, s_z + 6)

    def when_edge(e, fn):
        if e == 0:
            pl.when(has_up)(fn)
        elif e == nb + 1:
            pl.when(has_dn)(fn)
        else:
            fn()

    lane_h = lane_iota(hw)
    group_h = lane_h // (2 * hw)
    side_h = (lane_h // hw) % 2

    blocks = list(range(2, nb)) + [1, nb]
    order = blocks + [0, nb + 1]
    own_sl = mine(v)
    gains = []

    def ag_start(it, e):
        rcopy(fg.at[e, own_sl], fg.at[e, own_sl], it, ne + e, to_b).start()
        rcopy(fg.at[e, own_sl], fg.at[e, own_sl], it, e, to_a).start()

    def rims_start(it):
        @pl.when(has_dn)
        def _():
            rcopy(fg.at[nb, own_sl], fg.at[0, own_sl], it, s_yd, to_dn).start()

        @pl.when(has_up)
        def _():
            rcopy(fg.at[1, own_sl], fg.at[nb + 1, own_sl], it, s_yu, to_up).start()

    rims_start(0)
    for e in blocks:
        ag_start(0, e)

    for it in range(ITERS):

        def ag_forward(e):
            landed(fg.at[e, mine(vb)], it, ne + e, to_b)
            rcopy(fg.at[e, mine(vb)], fg.at[e, mine(vb)], it, 2 * ne + e, to_a).start()

        if it == 0:
            for vv in range(views):
                build_depth(mt, vv, taps[0, 3 * vv + 2 : 3 * vv + 3, :], rows_z, hw)
                build_plane_row(
                    am, vv * blk, taps[0, 3 * vv : 3 * vv + 1, :],
                    taps[0, 3 * vv + 1 : 3 * vv + 2, :], planes, hw,
                )

        @pl.when(has_up)
        def _():
            landed(fg.at[0, own_sl], it, s_yd, to_up)
            ag_start(it, 0)

        @pl.when(has_dn)
        def _():
            landed(fg.at[nb + 1, own_sl], it, s_yu, to_dn)
            ag_start(it, nb + 1)

        for e in range(ne):
            packed = jnp.zeros((hw, LANES), F32)
            for p in range(own):
                body = fg[e, own * v + p]
                first = roll_lanes(body[:, :LANES], 2 * hw * p + hw)
                last = roll_lanes(body[:, rows_z - LANES :], 2 * hw * p + hw)
                pair = jnp.where(side_h == 0, last, first)
                packed = jnp.where(group_h == p, pair, packed)
            wk[e] = packed

        @pl.when(has_lf)
        def _():
            rcopy(wk, wr, it, s_zl, to_lf).start()

        @pl.when(has_rt)
        def _():
            rcopy(wk, wl, it, s_zr, to_rt).start()

        ag_forward(blocks[0])

        if it == 0:
            for vv in range(views):
                build_plane_row(
                    bm.at[vv], 0, taps[1, 3 * vv : 3 * vv + 1, :],
                    taps[1, 3 * vv + 1 : 3 * vv + 2, :], planes, hw,
                )
            for vv in range(views):
                mid = planes // 2 * hw
                along_z = mt[vv, rows_z // 2 : rows_z // 2 + 1, :rows_z].astype(F32)
                along_z = jnp.sum(along_z, axis=1, keepdims=True)
                fwd = am[vv * blk + mid : vv * blk + mid + 1, :].astype(F32)
                bwd = bm[vv, mid : mid + 1, :].astype(F32)
                gain = 1.0 / (jnp.sum(bwd, axis=1, keepdims=True) * along_z)
                gains.append((jnp.sum(fwd, axis=1, keepdims=True) * along_z, gain))
                ones = jnp.sum(mt[vv].astype(F32), axis=0, keepdims=True) * gain
                g1[vv] = jnp.broadcast_to(ones, g1.shape[1:])
                for j in range(3):
                    part = bm[vv, :, j * blk : (j + 1) * blk].astype(F32)
                    part = jnp.sum(part, axis=1, keepdims=True)
                    rb[vv, j] = jnp.broadcast_to(part, rb.shape[2:])
            load.wait()

        @pl.when(has_lf)
        def _():
            landed(wl, it, s_zr, to_lf)

        @pl.when(has_rt)
        def _():
            landed(wr, it, s_zl, to_rt)

        for e in range(ne):
            pk[v, e] = jnp.where(side_h == 0, wl[e], wr[e])
        rcopy(pk.at[v], pk.at[v], it, s_p + 1, to_b).start()
        rcopy(pk.at[v], pk.at[v], it, s_p, to_a).start()

        have = set()

        def process(e):
            def arrivals():
                landed(fg.at[e, mine(va)], it, e, to_a)
                landed(fg.at[e, mine(vc)], it, 2 * ne + e, to_a)
            when_edge(e, arrivals)
            fb[e * blk : (e + 1) * blk, :rows_z] = fg[e].reshape(blk, rows_z).astype(BF)
            before = {b for b in range(nb) if {b, b + 1, b + 2} <= have}
            have.add(e)
            for b in range(nb):
                if b not in before and {b, b + 1, b + 2} <= have:
                    core = fb[b * blk : (b + 3) * blk, :rows_z]
                    gs[b] = jnp.dot(am[...], core, preferred_element_type=F32).astype(BF)

        for k in range(1, ne):
            when_edge(order[k], functools.partial(ag_forward, order[k]))
            process(order[k - 1])
        landed(pk.at[vb], it, s_p + 1, to_b)
        rcopy(pk.at[vb], pk.at[vb], it, s_p + 2, to_a).start()
        process(order[-1])
        landed(pk.at[va], it, s_p, to_a)
        landed(pk.at[vc], it, s_p + 2, to_a)

        @pl.loop(0, ne)
        def _(e):
            base = pl.multiple_of(e * blk, blk)
            for x in range(planes):
                rim = jnp.where(group_h == x % own, pk[x // own, e], 0.0)
                fb[pl.ds(base + x * hw, hw), rows_z:] = rim.astype(BF)

        @pl.loop(0, nb)
        def _(b):
            base = pl.multiple_of(b * blk, blk)
            edge = fb[pl.ds(base, 3 * blk), rows_z:]
            edge = jnp.dot(am[...], edge, preferred_element_type=F32).astype(BF)
            g = jnp.concatenate([gs[b], edge], axis=1)
            z_block = lax.broadcasted_iota(jnp.int32, (1, rows_z), 1) // BZ
            y_block = b * hw // BY
            for vv in range(views):
                scale = jnp.zeros((1, rows_z), F32)
                valid = jnp.zeros((1, rows_z), jnp.int32)
                for c in range(rows_z // BZ):
                    scale = jnp.where(z_block == c, scales[vv, y_block, c], scale)
                    valid = jnp.where(z_block == c, flags[vv, y_block, c], valid)
                blurred = lax.dot_general(
                    g[vv * blk : (vv + 1) * blk], mt[vv], (((1,), (1,)), ((), ())),
                    preferred_element_type=F32,
                )
                data = vd[vv, :, pl.ds(pl.multiple_of(b * hw, hw), hw), :].astype(F32)
                ratio = jnp.where(
                    valid == 1, data.reshape(blk, rows_z) * (scale * gains[vv][0]) / blurred - 1.0, 0.0
                )
                spread = jnp.dot(ratio.astype(BF), mt[vv], preferred_element_type=F32) * gains[vv][1]
                gp[vv, pl.ds(base + 2 * blk, blk), :] = spread.astype(BF)

        @pl.when(has_dn)
        def _():
            sent(fg.at[nb, own_sl], it, s_yd, to_dn)

        @pl.when(has_up)
        def _():
            sent(fg.at[1, own_sl], it, s_yu, to_up)

        @pl.when(has_lf)
        def _():
            sent(wk, it, s_zl, to_lf)

        @pl.when(has_rt)
        def _():
            sent(wk, it, s_zr, to_rt)

        for e in range(ne):
            def sends(e=e):
                sent(fg.at[e, own_sl], it, e, to_a)
                sent(fg.at[e, own_sl], it, ne + e, to_b)
                sent(fg.at[e, mine(vb)], it, 2 * ne + e, to_a)
            when_edge(e, sends)
        sent(pk.at[v], it, s_p, to_a)
        sent(pk.at[v], it, s_p + 1, to_b)
        sent(pk.at[vb], it, s_p + 2, to_a)

        def used(e):
            return ((e > 0) | has_up) & ((e < nb + 1) | has_dn)

        def r1_copy(e, k):
            owner = (va, vc)[k]
            return rcopy(ob.at[e, mine(owner)], r1.at[e, k], it, s_r1 + 2 * e + k, to_a)

        def back(e, lanes):
            rows = pl.ds(pl.multiple_of(e * blk, blk), 3 * blk)
            total = jnp.dot(bm[0], gp[0, rows, lanes], preferred_element_type=F32)
            for vv in range(1, views):
                total = total + jnp.dot(bm[vv], gp[vv, rows, lanes], preferred_element_type=F32)
            for vv in range(views):
                across = jnp.zeros((blk, LANES), F32)
                for j in range(3):
                    inside = (e + j >= 2) & (e + j < nb + 2)
                    across = across + rb[vv, j] * jnp.where(inside, 1.0, 0.0)
                row = g1[vv, 0:1, lanes]
                total = total + jnp.concatenate([across] * (row.shape[1] // LANES), axis=1) * row
            return total

        @pl.loop(0, ne)
        def _(e):
            @pl.when(used(e))
            def _():
                rims = back(e, slice(rows_z, None)).reshape(planes, hw, LANES)
                for o in range(planes // own):
                    packed = rims[own * o]
                    for p in range(1, own):
                        packed = jnp.where(group_h == p, rims[own * o + p], packed)
                    zp[o, e] = packed

        rcopy(zp.at[vc], r1z.at[1], it, s_z + 1, to_a).start()
        rcopy(zp.at[va], r1z.at[0], it, s_z, to_a).start()

        def nth(i):
            e = jnp.where(i == nb, 1, jnp.where(i == nb + 1, nb, i))
            return jnp.where(i == 0, 0, jnp.where(i == 1, nb + 1, e))

        @pl.loop(0, ne + 1)
        def _(i):
            e = nth(i)
            @pl.when((i < ne) & used(e))
            def _():
                ob[e] = back(e, slice(0, rows_z)).reshape(planes, hw, rows_z)
                r1_copy(e, 1).start()
                r1_copy(e, 0).start()

            @pl.when(i == 1)
            def _():
                landed(r1z.at[1], it, s_z + 1, to_a)
                s2z[...] = zp[vb] + r1z[1]
                rcopy(s2z, r2z, it, s_z + 2, to_b).start()

            q = nth(jnp.maximum(i - 1, 0))
            @pl.when((i > 0) & used(q))
            def _():
                r1_copy(q, 1).wait_recv()
                s2[q] = ob[q, mine(vb)] + r1[q, 1]
                rcopy(s2.at[q], r2.at[q], it, s_r2 + q, to_b).start()

        landed(r1z.at[0], it, s_z, to_a)
        landed(r2z, it, s_z + 2, to_b)
        zu[...] = zp[v] + r1z[0] + r2z[...]

        @pl.when(has_lf)
        def _():
            rcopy(zu, zr, it, s_rl, to_lf).start()

        @pl.when(has_rt)
        def _():
            rcopy(zu, zl, it, s_rr, to_rt).start()

        def gather_sum(e):
            r1_copy(e, 0).wait_recv()
            landed(r2.at[e], it, s_r2 + e, to_b)
            ub[e] = ob[e, own_sl] + r1[e, 0] + r2[e]

        def add_rims(e):
            for p in range(own):
                last = roll_lanes(zr[e], LANES - hw - 2 * hw * p)
                first = roll_lanes(zl[e], -(2 * hw * p + hw))
                ub[e, p, :, :LANES] += jnp.where(lane_h < hw, first, 0.0)
                ub[e, p, :, rows_z - LANES :] += jnp.where(lane_h >= LANES - hw, last, 0.0)

        for e in (0, nb + 1):
            when_edge(e, functools.partial(gather_sum, e))

        @pl.when(has_rt)
        def _():
            landed(zr, it, s_rl, to_rt)

        @pl.when(has_lf)
        def _():
            landed(zl, it, s_rr, to_lf)

        for e in (0, nb + 1):
            when_edge(e, functools.partial(add_rims, e))

        @pl.when(has_up)
        def _():
            rcopy(ub.at[0], yd, it, s_ru, to_up).start()

        @pl.when(has_dn)
        def _():
            rcopy(ub.at[nb + 1], yu, it, s_rd, to_dn).start()

        for e in blocks:
            gather_sum(e)
            add_rims(e)
            if e == 1:
                @pl.when(has_up)
                def _():
                    landed(yu, it, s_rd, to_up)
            if e == nb:
                @pl.when(has_dn)
                def _():
                    landed(yd, it, s_ru, to_dn)
            for p in range(own):
                total = ub[e, p]
                if e == 1:
                    total = total + yu[p]
                if e == nb:
                    total = total + yd[p]
                fresh = fg[e, own * v + p] * total / view_total
                if it + 1 < ITERS:
                    fg[e, own * v + p] = fresh
                else:
                    out[p, (e - 1) * hw : e * hw, :] = fresh
            if it + 1 < ITERS:
                ag_start(it + 1, e)
        if it + 1 < ITERS:
            rims_start(it + 1)

        @pl.loop(0, ne)
        def _(e):
            @pl.when(used(e))
            def _():
                r1_copy(e, 0).wait_send()
                r1_copy(e, 1).wait_send()
                sent(s2.at[e], it, s_r2 + e, to_b)

        sent(zp.at[va], it, s_z, to_a)
        sent(zp.at[vc], it, s_z + 1, to_a)
        sent(s2z, it, s_z + 2, to_b)

        @pl.when(has_lf)
        def _():
            sent(zu, it, s_rl, to_lf)

        @pl.when(has_rt)
        def _():
            sent(zu, it, s_rr, to_rt)

        @pl.when(has_up)
        def _():
            sent(ub.at[0], it, s_ru, to_up)

        @pl.when(has_dn)
        def _():
            sent(ub.at[nb + 1], it, s_rd, to_dn)


def per_device(ny, nz, estimate, view_data, block_scales, block_flags, profile, supports):
    views, planes, rows_y, rows_z = view_data.shape
    own = estimate.shape[0]
    hw = (profile.shape[2] - 1) // 2
    nb = rows_y // hw
    ne = nb + 2
    blk = planes * hw
    wide = rows_z + LANES
    forward = kernel_table(profile, supports)
    both = jnp.stack([forward, forward[:, :, ::-1]]).reshape(2, views * 3, profile.shape[2])
    taps = jnp.pad(both, ((0, 0), (0, 0), (0, LANES - profile.shape[2])))
    owners = planes // own
    n_sem = 6 * ne + 7 + 7
    vm = pltpu.VMEM
    scratch = [
        vm((ne, planes, hw, rows_z), F32),
        vm((owners, ne, hw, LANES), F32),
        vm((ne, hw, LANES), F32),
        vm((ne, hw, LANES), F32),
        vm((ne, hw, LANES), F32),
        vm((ne * blk, wide), BF),
        vm((views * blk, 3 * blk), BF),
        vm((views, blk, 3 * blk), BF),
        vm((views, rows_z, wide), BF),
        vm((views, (nb + 4) * blk, wide), BF),
        vm((ne, planes, hw, rows_z), F32),
        vm((owners, ne, hw, LANES), F32),
        vm((ne, 2, own, hw, rows_z), F32),
        vm((2, ne, hw, LANES), F32),
        vm((ne, own, hw, rows_z), F32),
        vm((ne, hw, LANES), F32),
        vm((ne, own, hw, rows_z), F32),
        vm((ne, hw, LANES), F32),
        vm((ne, own, hw, rows_z), F32),
        vm((ne, hw, LANES), F32),
        vm((ne, hw, LANES), F32),
        vm((ne, hw, LANES), F32),
        vm((own, hw, rows_z), F32),
        vm((own, hw, rows_z), F32),
        vm(view_data.shape, view_data.dtype),
        vm((views, 3, blk, LANES), F32),
        vm((views, 8, wide), F32),
        vm((nb, views * blk, rows_z), BF),
        pltpu.SemaphoreType.DMA,
        pltpu.SemaphoreType.DMA((ITERS, n_sem)),
        pltpu.SemaphoreType.DMA((ITERS, n_sem)),
    ]
    in_vm = pl.BlockSpec(memory_space=pltpu.VMEM)
    in_sm = pl.BlockSpec(memory_space=pltpu.SMEM)
    return pl.pallas_call(
        functools.partial(kernel, (ny, nz, views, planes, rows_y, rows_z, own, hw)),
        out_shape=jax.ShapeDtypeStruct(estimate.shape, F32),
        in_specs=[in_vm, pl.BlockSpec(memory_space=pl.ANY), in_sm, in_sm, in_vm],
        out_specs=in_vm,
        scratch_shapes=scratch,
        compiler_params=pltpu.CompilerParams(collective_id=0, has_side_effects=True),
    )(estimate, view_data, block_scales, block_flags, taps)


def solution(mesh):
    placed = (
        P("view", "gy", "gz"),
        P("view", None, "gy", "gz"),
        P("view", "gy", "gz"),
        P("view", "gy", "gz"),
        P("view", None, None),
        P("view", None),
    )
    body = functools.partial(per_device, mesh.shape["gy"], mesh.shape["gz"])
    return jax.shard_map(
        body, mesh=mesh, in_specs=placed, out_specs=P("view", "gy", "gz"), check_vma=False
    )
```

```python
import functools

import jax
import jax.numpy as jnp
from jax import lax
from jax.experimental import pallas as pl
from jax.experimental.pallas import tpu as pltpu
from jax.sharding import PartitionSpec as P

BY = 32
BZ = 64
ITERS = 2
LANES = 128
MESH = pl.DeviceIdType.MESH
BF = jnp.bfloat16
F32 = jnp.float32


def kernel_table(profile, supports):
    tap_count = profile.shape[-1]
    distance = jnp.abs(jnp.arange(tap_count, dtype=jnp.int32) - (tap_count - 1) // 2)
    inside = distance[None, None, :] <= supports[:, :, None]
    masked = jnp.where(inside, profile, 0.0)
    return masked / jnp.sum(masked, axis=-1, keepdims=True)


def lane_iota(rows):
    return lax.broadcasted_iota(jnp.int32, (rows, LANES), 1)


def toeplitz(row, rows, shift):
    wide = jnp.broadcast_to(row, (rows, LANES))
    return pltpu.roll(wide, shift % LANES, 1, stride=1, stride_axis=0)


def roll_lanes(x, shift):
    shift = shift % LANES
    return pltpu.roll(x, shift, 1) if shift else x


def build_plane_row(dst, row_base, kx, ky, planes, hw):
    lane = lane_iota(hw)
    per_tile = LANES // hw
    halves = planes // per_tile
    tall = toeplitz(ky, hw, 0)
    bands = []
    for d in range(3):
        q = jnp.where(lane < hw, roll_lanes(tall, -hw * d), 0.0)
        width = hw
        while width < LANES:
            q = q + roll_lanes(q, width)
            width *= 2
        bands.append(q)
    tx = toeplitz(kx, planes, -hw)
    row_id = lax.broadcasted_iota(jnp.int32, (LANES, LANES), 0)
    group = lax.broadcasted_iota(jnp.int32, (LANES, LANES), 1) // hw
    for half in range(halves):
        pick = (row_id == group + half * per_tile).astype(F32)
        spread = jnp.dot(tx, pick, precision=lax.Precision.HIGHEST, preferred_element_type=F32)
        for d in range(3):
            for x in range(planes):
                tile = spread[x : x + 1, :] * bands[d]
                c0 = (halves * d + half) * LANES
                dst[row_base + x * hw : row_base + (x + 1) * hw, c0 : c0 + LANES] = tile.astype(BF)


def build_depth(dst, v, kz, rows_z, hw):
    row_j = lax.broadcasted_iota(jnp.int32, (rows_z, LANES), 0)
    lane = lane_iota(rows_z)
    reps = rows_z // LANES
    t = jnp.concatenate([toeplitz(kz, LANES, -hw)] * reps, axis=0)
    for ct in range(reps):
        c = lane + ct * LANES
        keep = jnp.abs(c - row_j) <= hw
        dst[v, :, ct * LANES : (ct + 1) * LANES] = jnp.where(keep, t, 0.0).astype(BF)
    h = jnp.concatenate([toeplitz(kz, LANES, 0)] * reps, axis=0)
    low = (row_j < hw) & (lane < hw)
    high = (row_j >= rows_z - hw) & (lane >= hw) & (lane < 2 * hw)
    h = jnp.where(low | high, h, 0.0)
    width = 2 * hw
    while width < LANES:
        h = h + roll_lanes(h, width)
        width *= 2
    dst[v, :, rows_z : rows_z + LANES] = h.astype(BF)


def kernel(
    sizes, est, vd_any, scales, flags, taps, out,
    fg, pk, wk, wl, wr, fb, am, bm, mt, gp, ob, zp,
    r1, r1z, s2, s2z, r2, r2z, ub, zu, zl, zr, yu, yd, vd, rb, g1, gs, dsem, ssem, rsem,
):
    ny, nz, views, planes, rows_y, rows_z, own, hw = sizes
    nb = rows_y // hw
    ne = nb + 2
    blk = planes * hw
    v = lax.axis_index("view")
    gy = lax.axis_index("gy")
    gz = lax.axis_index("gz")
    va, vb, vc = (lax.bitwise_xor(v, 1), lax.bitwise_xor(v, 2), lax.bitwise_xor(v, 3))
    has_up, has_dn = (gy > 0, gy < ny - 1)
    has_lf, has_rt = (gz > 0, gz < nz - 1)
    to_a, to_b = ({"view": va}, {"view": vb})
    to_up, to_dn = ({"gy": jnp.maximum(gy - 1, 0)}, {"gy": jnp.minimum(gy + 1, ny - 1)})
    to_lf, to_rt = ({"gz": jnp.maximum(gz - 1, 0)}, {"gz": jnp.minimum(gz + 1, nz - 1)})
    view_total = views * 4

    def mine(o):
        return pl.ds(o * own, own)

    def rcopy(src, dst, it, sid, dev):
        return pltpu.make_async_remote_copy(
            src_ref=src, dst_ref=dst, send_sem=ssem.at[it, sid], recv_sem=rsem.at[it, sid],
            device_id=dev, device_id_type=MESH,
        )

    def landed(dst, it, sid, dev):
        rcopy(dst, dst, it, sid, dev).wait_recv()

    def sent(src, it, sid, dev):
        rcopy(src, src, it, sid, dev).wait_send()

    load = pltpu.make_async_copy(vd_any, vd, dsem)
    load.start()
    for ref in (wl, wr, zl, zr, yu, yd, zp):
        ref[...] = jnp.zeros_like(ref)
    for e in (0, nb + 1):
        fg[e] = jnp.zeros((planes, hw, rows_z), F32)
    for vv in range(views):
        for e in (0, 1, nb + 2, nb + 3):
            gp[vv, e * blk : (e + 1) * blk, :] = jnp.zeros((blk, rows_z + LANES), BF)
    for b in range(nb):
        for p in range(own):
            fg[1 + b, own * v + p] = est[p, b * hw : (b + 1) * hw, :]

    barrier = pltpu.get_barrier_semaphore()
    for dev in (to_a, to_b):
        pl.semaphore_signal(barrier, inc=1, device_id=dev, device_id_type=MESH)
    for cond, dev in ((has_up, to_up), (has_dn, to_dn), (has_lf, to_lf), (has_rt, to_rt)):
        @pl.when(cond)
        def _():
            pl.semaphore_signal(barrier, inc=1, device_id=dev, device_id_type=MESH)
    sides = [c.astype(jnp.int32) for c in (has_up, has_dn, has_lf, has_rt)]
    pl.semaphore_wait(barrier, 2 + sides[0] + sides[1] + sides[2] + sides[3])

    s_p = 3 * ne
    s_yu, s_yd, s_zl, s_zr = (3 * ne + 3, 3 * ne + 4, 3 * ne + 5, 3 * ne + 6)
    s_r1 = 3 * ne + 7
    s_r2 = s_r1 + 2 * ne
    s_z = s_r2 + ne
    s_rl, s_rr, s_ru, s_rd = (s_z + 3, s_z + 4, s_z + 5, s_z + 6)

    def when_edge(e, fn):
        if e == 0:
            pl.when(has_up)(fn)
        elif e == nb + 1:
            pl.when(has_dn)(fn)
        else:
            fn()

    lane_h = lane_iota(hw)
    group_h = lane_h // (2 * hw)
    side_h = (lane_h // hw) % 2

    blocks = list(range(2, nb)) + [1, nb]
    order = blocks + [0, nb + 1]
    own_sl = mine(v)
    gains = []

    def ag_start(it, e):
        rcopy(fg.at[e, own_sl], fg.at[e, own_sl], it, ne + e, to_b).start()
        rcopy(fg.at[e, own_sl], fg.at[e, own_sl], it, e, to_a).start()

    def rims_start(it):
        @pl.when(has_dn)
        def _():
            rcopy(fg.at[nb, own_sl], fg.at[0, own_sl], it, s_yd, to_dn).start()

        @pl.when(has_up)
        def _():
            rcopy(fg.at[1, own_sl], fg.at[nb + 1, own_sl], it, s_yu, to_up).start()

    rims_start(0)
    for e in blocks:
        ag_start(0, e)

    for it in range(ITERS):

        def ag_forward(e):
            landed(fg.at[e, mine(vb)], it, ne + e, to_b)
            rcopy(fg.at[e, mine(vb)], fg.at[e, mine(vb)], it, 2 * ne + e, to_a).start()

        if it == 0:
            for vv in range(views):
                build_depth(mt, vv, taps[0, 3 * vv + 2 : 3 * vv + 3, :], rows_z, hw)
                build_plane_row(
                    am, vv * blk, taps[0, 3 * vv : 3 * vv + 1, :],
                    taps[0, 3 * vv + 1 : 3 * vv + 2, :], planes, hw,
                )

        @pl.when(has_up)
        def _():
            landed(fg.at[0, own_sl], it, s_yd, to_up)
            ag_start(it, 0)

        @pl.when(has_dn)
        def _():
            landed(fg.at[nb + 1, own_sl], it, s_yu, to_dn)
            ag_start(it, nb + 1)

        for e in range(ne):
            packed = jnp.zeros((hw, LANES), F32)
            for p in range(own):
                body = fg[e, own * v + p]
                first = roll_lanes(body[:, :LANES], 2 * hw * p + hw)
                last = roll_lanes(body[:, rows_z - LANES :], 2 * hw * p + hw)
                pair = jnp.where(side_h == 0, last, first)
                packed = jnp.where(group_h == p, pair, packed)
            wk[e] = packed

        @pl.when(has_lf)
        def _():
            rcopy(wk, wr, it, s_zl, to_lf).start()

        @pl.when(has_rt)
        def _():
            rcopy(wk, wl, it, s_zr, to_rt).start()

        ag_forward(blocks[0])


        @pl.when(has_lf)
        def _():
            landed(wl, it, s_zr, to_lf)

        @pl.when(has_rt)
        def _():
            landed(wr, it, s_zl, to_rt)

        for e in range(ne):
            pk[v, e] = jnp.where(side_h == 0, wl[e], wr[e])
        rcopy(pk.at[v], pk.at[v], it, s_p + 1, to_b).start()
        rcopy(pk.at[v], pk.at[v], it, s_p, to_a).start()

        def build_back(vv):
            build_plane_row(
                bm.at[vv], 0, taps[1, 3 * vv : 3 * vv + 1, :],
                taps[1, 3 * vv + 1 : 3 * vv + 2, :], planes, hw,
            )

        def sum_tables(vv):
            mid = planes // 2 * hw
            along_z = mt[vv, rows_z // 2 : rows_z // 2 + 1, :rows_z].astype(F32)
            along_z = jnp.sum(along_z, axis=1, keepdims=True)
            fwd = am[vv * blk + mid : vv * blk + mid + 1, :].astype(F32)
            bwd = bm[vv, mid : mid + 1, :].astype(F32)
            gain = 1.0 / (jnp.sum(bwd, axis=1, keepdims=True) * along_z)
            gains.append((jnp.sum(fwd, axis=1, keepdims=True) * along_z, gain))
            ones = jnp.sum(mt[vv].astype(F32), axis=0, keepdims=True) * gain
            g1[vv] = jnp.broadcast_to(ones, g1.shape[1:])
            parts = []
            for j in range(3):
                part = bm[vv, :, j * blk : (j + 1) * blk].astype(F32)
                part = jnp.sum(part, axis=1, keepdims=True)
                parts.append(jnp.broadcast_to(part, rb.shape[2:]))
            for e in range(ne):
                rb[e, vv] = sum(parts[j] for j in range(3) if 2 <= e + j < nb + 2)

        tasks = []
        if it == 0:
            for vv in range(views):
                tasks.append(functools.partial(build_back, vv))
                tasks.append(functools.partial(sum_tables, vv))

        have = set()

        def process(e):
            def arrivals():
                landed(fg.at[e, mine(va)], it, e, to_a)
                landed(fg.at[e, mine(vc)], it, 2 * ne + e, to_a)
            when_edge(e, arrivals)
            fb[e * blk : (e + 1) * blk, :rows_z] = fg[e].reshape(blk, rows_z).astype(BF)
            before = {b for b in range(nb) if {b, b + 1, b + 2} <= have}
            have.add(e)
            for b in range(nb):
                if b not in before and {b, b + 1, b + 2} <= have:
                    core = fb[b * blk : (b + 3) * blk, :rows_z]
                    gs[b] = jnp.dot(am[...], core, preferred_element_type=F32).astype(BF)

        for k in range(1, ne):
            when_edge(order[k], functools.partial(ag_forward, order[k]))
            process(order[k - 1])
            if tasks:
                tasks.pop(0)()
        for task in tasks:
            task()
        if it == 0:
            load.wait()
        landed(pk.at[vb], it, s_p + 1, to_b)
        rcopy(pk.at[vb], pk.at[vb], it, s_p + 2, to_a).start()
        process(order[-1])
        landed(pk.at[va], it, s_p, to_a)
        landed(pk.at[vc], it, s_p + 2, to_a)

        @pl.loop(0, ne)
        def _(e):
            base = pl.multiple_of(e * blk, blk)
            for x in range(planes):
                rim = jnp.where(group_h == x % own, pk[x // own, e], 0.0)
                fb[pl.ds(base + x * hw, hw), rows_z:] = rim.astype(BF)

        @pl.loop(0, nb)
        def _(b):
            base = pl.multiple_of(b * blk, blk)
            edge = fb[pl.ds(base, 3 * blk), rows_z:]
            edge = jnp.dot(am[...], edge, preferred_element_type=F32).astype(BF)
            g = jnp.concatenate([gs[b], edge], axis=1)
            z_block = lax.broadcasted_iota(jnp.int32, (1, rows_z), 1) // BZ
            y_block = b * hw // BY
            for vv in range(views):
                scale = jnp.zeros((1, rows_z), F32)
                valid = jnp.zeros((1, rows_z), jnp.int32)
                for c in range(rows_z // BZ):
                    scale = jnp.where(z_block == c, scales[vv, y_block, c], scale)
                    valid = jnp.where(z_block == c, flags[vv, y_block, c], valid)
                blurred = lax.dot_general(
                    g[vv * blk : (vv + 1) * blk], mt[vv], (((1,), (1,)), ((), ())),
                    preferred_element_type=F32,
                )
                data = vd[vv, :, pl.ds(pl.multiple_of(b * hw, hw), hw), :].astype(F32)
                ratio = jnp.where(
                    valid == 1, data.reshape(blk, rows_z) * (scale * gains[vv][0]) / blurred - 1.0, 0.0
                )
                spread = jnp.dot(ratio.astype(BF), mt[vv], preferred_element_type=F32) * gains[vv][1]
                gp[vv, pl.ds(base + 2 * blk, blk), :] = spread.astype(BF)

        @pl.when(has_dn)
        def _():
            sent(fg.at[nb, own_sl], it, s_yd, to_dn)

        @pl.when(has_up)
        def _():
            sent(fg.at[1, own_sl], it, s_yu, to_up)

        @pl.when(has_lf)
        def _():
            sent(wk, it, s_zl, to_lf)

        @pl.when(has_rt)
        def _():
            sent(wk, it, s_zr, to_rt)

        for e in range(ne):
            def sends(e=e):
                sent(fg.at[e, own_sl], it, e, to_a)
                sent(fg.at[e, own_sl], it, ne + e, to_b)
                sent(fg.at[e, mine(vb)], it, 2 * ne + e, to_a)
            when_edge(e, sends)
        sent(pk.at[v], it, s_p, to_a)
        sent(pk.at[v], it, s_p + 1, to_b)
        sent(pk.at[vb], it, s_p + 2, to_a)

        def used(e):
            return ((e > 0) | has_up) & ((e < nb + 1) | has_dn)

        def r1_copy(e, k):
            owner = (va, vc)[k]
            return rcopy(ob.at[e, mine(owner)], r1.at[e, k], it, s_r1 + 2 * e + k, to_a)

        def back(e, lanes):
            rows = pl.ds(pl.multiple_of(e * blk, blk), 3 * blk)
            total = jnp.dot(bm[0], gp[0, rows, lanes], preferred_element_type=F32)
            for vv in range(1, views):
                total = total + jnp.dot(bm[vv], gp[vv, rows, lanes], preferred_element_type=F32)
            for vv in range(views):
                across = rb[e, vv]
                row = g1[vv, 0:1, lanes]
                total = total + jnp.concatenate([across] * (row.shape[1] // LANES), axis=1) * row
            return total

        @pl.loop(0, ne)
        def _(e):
            @pl.when(used(e))
            def _():
                rims = back(e, slice(rows_z, None)).reshape(planes, hw, LANES)
                for o in range(planes // own):
                    packed = rims[own * o]
                    for p in range(1, own):
                        packed = jnp.where(group_h == p, rims[own * o + p], packed)
                    zp[o, e] = packed

        rcopy(zp.at[vc], r1z.at[1], it, s_z + 1, to_a).start()
        rcopy(zp.at[va], r1z.at[0], it, s_z, to_a).start()

        def nth(i):
            e = jnp.where(i == nb, 1, jnp.where(i == nb + 1, nb, i))
            return jnp.where(i == 0, 0, jnp.where(i == 1, nb + 1, e))

        @pl.loop(0, ne + 1)
        def _(i):
            e = nth(i)
            @pl.when((i < ne) & used(e))
            def _():
                ob[e] = back(e, slice(0, rows_z)).reshape(planes, hw, rows_z)
                r1_copy(e, 1).start()
                r1_copy(e, 0).start()

            @pl.when(i == 1)
            def _():
                landed(r1z.at[1], it, s_z + 1, to_a)
                s2z[...] = zp[vb] + r1z[1]
                rcopy(s2z, r2z, it, s_z + 2, to_b).start()

            q = nth(jnp.maximum(i - 1, 0))
            @pl.when((i > 0) & used(q))
            def _():
                r1_copy(q, 1).wait_recv()
                s2[q] = ob[q, mine(vb)] + r1[q, 1]
                rcopy(s2.at[q], r2.at[q], it, s_r2 + q, to_b).start()

        landed(r1z.at[0], it, s_z, to_a)
        landed(r2z, it, s_z + 2, to_b)
        zu[...] = zp[v] + r1z[0] + r2z[...]

        @pl.when(has_lf)
        def _():
            rcopy(zu, zr, it, s_rl, to_lf).start()

        @pl.when(has_rt)
        def _():
            rcopy(zu, zl, it, s_rr, to_rt).start()

        def gather_sum(e):
            r1_copy(e, 0).wait_recv()
            landed(r2.at[e], it, s_r2 + e, to_b)
            ub[e] = ob[e, own_sl] + r1[e, 0] + r2[e]

        def add_rims(e):
            for p in range(own):
                last = roll_lanes(zr[e], LANES - hw - 2 * hw * p)
                first = roll_lanes(zl[e], -(2 * hw * p + hw))
                ub[e, p, :, :LANES] += jnp.where(lane_h < hw, first, 0.0)
                ub[e, p, :, rows_z - LANES :] += jnp.where(lane_h >= LANES - hw, last, 0.0)

        for e in (0, nb + 1):
            when_edge(e, functools.partial(gather_sum, e))

        @pl.when(has_rt)
        def _():
            landed(zr, it, s_rl, to_rt)

        @pl.when(has_lf)
        def _():
            landed(zl, it, s_rr, to_lf)

        for e in (0, nb + 1):
            when_edge(e, functools.partial(add_rims, e))

        @pl.when(has_up)
        def _():
            rcopy(ub.at[0], yd, it, s_ru, to_up).start()

        @pl.when(has_dn)
        def _():
            rcopy(ub.at[nb + 1], yu, it, s_rd, to_dn).start()

        for e in blocks:
            gather_sum(e)
            add_rims(e)
            if e == 1:
                @pl.when(has_up)
                def _():
                    landed(yu, it, s_rd, to_up)
            if e == nb:
                @pl.when(has_dn)
                def _():
                    landed(yd, it, s_ru, to_dn)
            for p in range(own):
                total = ub[e, p]
                if e == 1:
                    total = total + yu[p]
                if e == nb:
                    total = total + yd[p]
                fresh = fg[e, own * v + p] * total / view_total
                if it + 1 < ITERS:
                    fg[e, own * v + p] = fresh
                else:
                    out[p, (e - 1) * hw : e * hw, :] = fresh
            if it + 1 < ITERS:
                ag_start(it + 1, e)
        if it + 1 < ITERS:
            rims_start(it + 1)

        @pl.loop(0, ne)
        def _(e):
            @pl.when(used(e))
            def _():
                r1_copy(e, 0).wait_send()
                r1_copy(e, 1).wait_send()
                sent(s2.at[e], it, s_r2 + e, to_b)

        sent(zp.at[va], it, s_z, to_a)
        sent(zp.at[vc], it, s_z + 1, to_a)
        sent(s2z, it, s_z + 2, to_b)

        @pl.when(has_lf)
        def _():
            sent(zu, it, s_rl, to_lf)

        @pl.when(has_rt)
        def _():
            sent(zu, it, s_rr, to_rt)

        @pl.when(has_up)
        def _():
            sent(ub.at[0], it, s_ru, to_up)

        @pl.when(has_dn)
        def _():
            sent(ub.at[nb + 1], it, s_rd, to_dn)


def per_device(ny, nz, estimate, view_data, block_scales, block_flags, profile, supports):
    views, planes, rows_y, rows_z = view_data.shape
    own = estimate.shape[0]
    hw = (profile.shape[2] - 1) // 2
    nb = rows_y // hw
    ne = nb + 2
    blk = planes * hw
    wide = rows_z + LANES
    forward = kernel_table(profile, supports)
    both = jnp.stack([forward, forward[:, :, ::-1]]).reshape(2, views * 3, profile.shape[2])
    taps = jnp.pad(both, ((0, 0), (0, 0), (0, LANES - profile.shape[2])))
    owners = planes // own
    n_sem = 6 * ne + 7 + 7
    vm = pltpu.VMEM
    scratch = [
        vm((ne, planes, hw, rows_z), F32),
        vm((owners, ne, hw, LANES), F32),
        vm((ne, hw, LANES), F32),
        vm((ne, hw, LANES), F32),
        vm((ne, hw, LANES), F32),
        vm((ne * blk, wide), BF),
        vm((views * blk, 3 * blk), BF),
        vm((views, blk, 3 * blk), BF),
        vm((views, rows_z, wide), BF),
        vm((views, (nb + 4) * blk, wide), BF),
        vm((ne, planes, hw, rows_z), F32),
        vm((owners, ne, hw, LANES), F32),
        vm((ne, 2, own, hw, rows_z), F32),
        vm((2, ne, hw, LANES), F32),
        vm((ne, own, hw, rows_z), F32),
        vm((ne, hw, LANES), F32),
        vm((ne, own, hw, rows_z), F32),
        vm((ne, hw, LANES), F32),
        vm((ne, own, hw, rows_z), F32),
        vm((ne, hw, LANES), F32),
        vm((ne, hw, LANES), F32),
        vm((ne, hw, LANES), F32),
        vm((own, hw, rows_z), F32),
        vm((own, hw, rows_z), F32),
        vm(view_data.shape, view_data.dtype),
        vm((ne, views, blk, LANES), F32),
        vm((views, 8, wide), F32),
        vm((nb, views * blk, rows_z), BF),
        pltpu.SemaphoreType.DMA,
        pltpu.SemaphoreType.DMA((ITERS, n_sem)),
        pltpu.SemaphoreType.DMA((ITERS, n_sem)),
    ]
    in_vm = pl.BlockSpec(memory_space=pltpu.VMEM)
    in_sm = pl.BlockSpec(memory_space=pltpu.SMEM)
    return pl.pallas_call(
        functools.partial(kernel, (ny, nz, views, planes, rows_y, rows_z, own, hw)),
        out_shape=jax.ShapeDtypeStruct(estimate.shape, F32),
        in_specs=[in_vm, pl.BlockSpec(memory_space=pl.ANY), in_sm, in_sm, in_vm],
        out_specs=in_vm,
        scratch_shapes=scratch,
        compiler_params=pltpu.CompilerParams(collective_id=0, has_side_effects=True),
    )(estimate, view_data, block_scales, block_flags, taps)


def solution(mesh):
    placed = (
        P("view", "gy", "gz"),
        P("view", None, "gy", "gz"),
        P("view", "gy", "gz"),
        P("view", "gy", "gz"),
        P("view", None, None),
        P("view", None),
    )
    body = functools.partial(per_device, mesh.shape["gy"], mesh.shape["gz"])
    return jax.shard_map(
        body, mesh=mesh, in_specs=placed, out_specs=P("view", "gy", "gz"), check_vma=False
    )
```
